32 devices in a mesh: gx: 2 (over core), gy: 4 (over y, x), gz: 4 (over z).
Axes of the slice: x: 2, y: 2, z: 4, core: 2. Of those that a mesh axis runs over, the one named last changes fastest.
Arguments:
- features: bfloat16 [4096, 512], P(('gx', 'gy', 'gz')), may hold values from -6 to 6
- halo_index: int32 [3072], P(('gx', 'gy', 'gz')), may hold values from 0 to 127
- edge_src: int32 [128, 384], P(('gx', 'gy', 'gz')), may hold values from 0 to 2623
- edge_dst: int32 [128, 384], P(('gx', 'gy', 'gz')), may hold values from 0 to 127
- edge_count: int32 [128], P(('gx', 'gy', 'gz')), may hold values from 48 to 384, as said below
- edge_basis: bfloat16 [49152, 128], P(('gx', 'gy', 'gz')), may hold values from -6 to 6
- w_edge_in: bfloat16 [4, 1152, 1024], P('gz'), may hold values from -0.1875 to 0.1875
- w_edge_out: bfloat16 [4, 1024, 512], P('gz'), may hold values from -0.1875 to 0.1875
- w_update: bfloat16 [512, 512], replicated, may hold values from -0.25 to 0.25
Outputs:
- new_features: bfloat16 [4096, 512], P(('gx', 'gy', 'gz'))
- halo_next: bfloat16 [832, 96, 512], P(('gx', 'gy', 'gz'))
The draws below stay inside these ranges and needn't reach their ends.
Inputs may be any that keep to these rules, and one draw needn't show every extreme that they name: The first edge_count slots of a domain's 384 slots for a species pair are live; in every draw some species pair has all 384 slots live in every domain of one gz group.
All inputs are finite; a program needn't handle non-finite values.
Results may differ from the reference program's by a relative error of at most 0.0051.
Values may be sent and summed in bfloat16 or wider, within the bound.
A program may use at most 128 MiB of HBM per device.

```python
import jax
import jax.numpy as jnp
from jax import lax

D = 512
HID = 1024
RB = 128
ATOM_DEV = 128
CAP = 384
HALO = 96
TABLE = 2624
TYPES = 4
ATOMS = 4096
N_GX = 2
N_GY = 4
N_GZ = 4
DEVICES = 32


def draw_edge_count(key, part):
    key_counts, key_group, key_helper = jax.random.split(key, 3)
    counts = jax.random.randint(key_counts, (DEVICES, N_GZ), CAP // 8, CAP + 1)
    group = jax.random.randint(key_group, (), 0, DEVICES // N_GZ)
    helper = jax.random.randint(key_helper, (), 0, N_GZ)
    rows = lax.broadcasted_iota(jnp.int32, (DEVICES, N_GZ), 0) // N_GZ
    columns = lax.broadcasted_iota(jnp.int32, (DEVICES, N_GZ), 1)
    filled = (rows == group) & (columns == helper)
    return jnp.where(filled, CAP, counts).reshape(DEVICES * N_GZ).astype(jnp.int32)


def set_ends(drawn, own_key, least, top_value):
    dims = drawn.shape
    spot = [jax.random.randint(jax.random.fold_in(own_key, axis), (), 0, dims[axis]) for axis in range(len(dims))]
    drawn = drawn.at[tuple(spot)].set(least)
    longest = dims.index(max(dims))
    spot[longest] = (spot[longest] + 1) % dims[longest]
    return drawn.at[tuple(spot)].set(top_value)


def levels(key, dims, cuts, smallest, top_value):
    def one(position, parts):
        draws = jax.random.uniform(jax.random.fold_in(jax.random.fold_in(key, 6), position), (parts,), jnp.float32, smallest / len(cuts), top_value / len(cuts))
        return jnp.repeat(jnp.exp(draws), dims[position] // parts).reshape((-1,) + (1,) * (len(dims) - position - 1))

    factor_of = one(*cuts[0])
    for cut in cuts[1:]:
        factor_of = factor_of * one(*cut)
    return factor_of


def normal_values(key, dims, width, reach, cuts=(), held_as=jnp.bfloat16):
    result = jax.random.normal(key, dims, jnp.float32) * width
    if len(cuts) > 0:
        result = levels(key, dims, cuts, -0.22, 0.18) * result
    return jnp.clip(result, min=-reach, max=reach).astype(held_as)


def setup_inputs(seed: int = 0) -> dict:
    key_of = jax.random.split(jax.random.key(seed), 10)
    features = normal_values(key_of[0], (ATOMS, D), 1.0, 6.0, ((0, 32),))
    halo_index = set_ends(jax.random.randint(key_of[1], (DEVICES * HALO,), 0, ATOM_DEV), jax.random.fold_in(key_of[1], 1), 0, ATOM_DEV - 1).astype(jnp.int32)
    edge_src = set_ends(jax.random.randint(key_of[2], (DEVICES * N_GZ, CAP), 0, TABLE), jax.random.fold_in(key_of[2], 1), 0, TABLE - 1).astype(jnp.int32)
    edge_dst = set_ends(jax.random.randint(key_of[3], (DEVICES * N_GZ, CAP), 0, ATOM_DEV), jax.random.fold_in(key_of[3], 1), 0, ATOM_DEV - 1).astype(jnp.int32)
    edge_count = draw_edge_count(jax.random.fold_in(key_of[9], 71), 0)
    edge_basis = normal_values(key_of[5], (DEVICES * N_GZ * CAP, RB), 1.0, 6.0, ((0, 32),))
    w_edge_in = normal_values(key_of[6], (TYPES, 2 * D + RB, HID), (2 * D + RB) ** -0.5, 0.1875, ((0, 4),))
    w_edge_out = normal_values(key_of[7], (TYPES, HID, D), HID ** -0.5, 0.1875, ((0, 4),))
    w_update = normal_values(key_of[8], (D, D), D ** -0.5, 0.25)
    return dict(features=features, halo_index=halo_index, edge_src=edge_src, edge_dst=edge_dst, edge_count=edge_count, edge_basis=edge_basis, w_edge_in=w_edge_in, w_edge_out=w_edge_out, w_update=w_update)


def neighbour_blocks(values, halo_index):
    boundary = jnp.take_along_axis(values, halo_index.reshape(DEVICES, HALO)[:, :, None], axis=1)
    boundary = boundary.reshape(N_GX, N_GY, N_GZ, HALO, D)
    blocks = []
    for shift_x in range(3):
        for shift_y in range(3):
            for shift_z in range(3):
                if shift_x == 1 and shift_y == 1 and (shift_z == 1):
                    continue
                blocks.append(jnp.roll(boundary, (1 - shift_x, 1 - shift_y, 1 - shift_z), axis=(0, 1, 2)))
    return jnp.stack(blocks, axis=3).reshape(DEVICES, 26 * HALO, D)

def reference(features, halo_index, edge_src, edge_dst, edge_count, edge_basis, w_edge_in, w_edge_out, w_update):
    own_rows = features.reshape(DEVICES, ATOM_DEV, D)
    table = jnp.concatenate([own_rows, neighbour_blocks(own_rows, halo_index)], axis=1)
    first_layer = w_edge_in.astype(jnp.float32)
    second_layer = w_edge_out.astype(jnp.float32)
    sources = edge_src.reshape(DEVICES, N_GZ, CAP)
    targets = edge_dst.reshape(DEVICES, N_GZ, CAP)
    counts = edge_count.reshape(DEVICES, N_GZ)
    basis = edge_basis.reshape(DEVICES, N_GZ, CAP, RB)

    def one_domain(items):
        table_rows, src_rows, dst_rows, count_rows, basis_rows = items
        inputs = jnp.concatenate([table_rows[src_rows], table_rows[dst_rows], basis_rows], axis=-1).astype(jnp.float32)
        pre = jnp.einsum('jck,jkh->jch', inputs, first_layer)
        hidden = lax.optimization_barrier(jax.nn.silu(pre).astype(jnp.bfloat16)).astype(jnp.float32)
        message = jnp.einsum('jch,jhd->jcd', hidden, second_layer).astype(jnp.bfloat16)
        message = lax.optimization_barrier(message).astype(jnp.float32)
        live = jnp.arange(CAP, dtype=jnp.int32)[None, :] < count_rows[:, None]
        message = jnp.where(live[:, :, None], message, jnp.float32(0.0))
        return jax.ops.segment_sum(message.reshape(-1, D), dst_rows.reshape(-1), num_segments=ATOM_DEV)
    aggregate = lax.map(one_domain, (table, sources, targets, counts, basis))
    normed = aggregate * lax.rsqrt(lax.optimization_barrier(jnp.mean(aggregate * aggregate, axis=-1, keepdims=True)) + 1e-05)
    normed = normed.astype(jnp.bfloat16).reshape(ATOMS, D)
    update = jnp.dot(normed, w_update, preferred_element_type=jnp.float32)
    new_features = (features.astype(jnp.float32) + update).astype(jnp.bfloat16)
    halo_next = neighbour_blocks(new_features.reshape(DEVICES, ATOM_DEV, D), halo_index)
    return (new_features, halo_next.reshape(DEVICES * 26, HALO, D))
```

```python
import functools

import jax
import jax.numpy as jnp
from jax import lax
from jax.experimental import pallas as pl
from jax.experimental.pallas import tpu as pltpu
from jax.sharding import PartitionSpec as P

AXES = ("gx", "gy", "gz")
MESH = pl.DeviceIdType.MESH


class Place:
    def __init__(self, sizes):
        self.nx, self.ny, self.nz = sizes
        self.x, self.y, self.z = (lax.axis_index(name) for name in AXES)
        x, y, z = self.x, self.y, self.z
        self.first = (x, y + 1 - 2 * lax.rem(y, 2), z)
        self.second = (x, lax.rem(y + 2, 4), z)
        self.b_first = 2 - 2 * lax.rem(y, 2)
        self.b_second = 2 * lax.rem(y, 2)
        self.siblings = [(lax.rem(x + 1, self.nx), y, z)]
        if self.nx > 2:
            self.siblings.append((lax.rem(x + self.nx - 1, self.nx), y, z))

    def along_z(self, step):
        return (self.x, self.y, lax.rem(self.z + step + self.nz, self.nz))

    def sibling_slot(self, index):
        return 1 if self.nx == 2 else 2 - index

    def meet(self):
        barrier = pltpu.get_barrier_semaphore()
        partners = [self.along_z(step) for step in range(1, self.nz)]
        partners += [self.first, self.second] + self.siblings
        for partner in partners:
            pl.semaphore_signal(barrier, inc=1, device_id=partner, device_id_type=MESH)
        pl.semaphore_wait(barrier, len(partners))


def remote(source, target, send, receive, device):
    return pltpu.make_async_remote_copy(
        src_ref=source,
        dst_ref=target,
        send_sem=send,
        recv_sem=receive,
        device_id=device,
        device_id_type=MESH,
    )


def gather_kernel(sizes, f_ref, h_ref, basis_ref, meta_ref, g_ref, hg_ref, bg_ref, mg_ref,
                  send, receive, e_send, e_receive, local):
    place = Place(sizes)
    z, nz = place.z, place.nz
    pairs = ((f_ref, g_ref), (h_ref, hg_ref))
    edge_pairs = ((meta_ref, mg_ref), (basis_ref, bg_ref))

    locals_ = []
    for q, (own, grid) in enumerate(pairs):
        locals_.append(pltpu.make_async_copy(own, grid.at[0, 1, z], local.at[q]))
    for q, (own, grid) in enumerate(edge_pairs):
        locals_.append(pltpu.make_async_copy(own.at[z], grid.at[z], local.at[2 + q]))
    for copy in locals_:
        copy.start()
    place.meet()

    entries = [(0, 0)] + [(s, sign) for s in range(1, nz) for sign in (-1, 1)]

    def when(entry, action):
        s, sign = entry
        zz = z + sign * s
        if s == 0:
            action(zz)
        else:
            pl.when((zz >= 0) & (zz < nz))(functools.partial(action, zz))

    def transfers(s, b, zz, kind, slot, device):
        out = []
        for q, (own, grid) in enumerate(pairs):
            source = own if (s == 0 and kind != 2 and b is None) else grid.at[0, 1 if b is None else b, zz]
            index = 1 if b is None else b
            out.append(remote(source, grid.at[slot[0], slot[1], zz], send.at[q, kind, index, zz],
                              receive.at[q, slot[0], slot[1], zz], device))
        return out

    def to_siblings(s, b, zz):
        out = []
        for i, device in enumerate(place.siblings):
            slot = (place.sibling_slot(i), 1 if b is None else b)
            out += transfers(s, b, zz, 4 + i, slot, device)
        return out

    def arrival(a, b, zz):
        for q, (own, grid) in enumerate(pairs):
            remote(grid.at[a, b, zz], grid.at[a, b, zz], send.at[q, 0, 0, 0],
                   receive.at[q, a, b, zz], place.first).wait_recv()

    def chain(entry, zz, do):
        s, sign = entry
        if s < nz - 1:
            for go in ((1, -1) if s == 0 else (-sign,)):
                device = (place.x, place.y, z + go)

                def act():
                    for copy in transfers(s, None, zz, 0 if go > 0 else 1, (0, 1), device):
                        do(copy)

                pl.when((z + go >= 0) & (z + go < nz))(act)

    def own_stage(entry, do):
        def act(zz):
            if entry[0] > 0 and do is start:
                arrival(0, 1, zz)
            chain(entry, zz, do)
            for copy in transfers(entry[0], None, zz, 2 if entry[0] > 0 else 3, (0, 2 - place.b_first), place.first):
                do(copy)
            for copy in to_siblings(entry[0], None, zz):
                do(copy)

        when(entry, act)

    def first_stage(entry, do):
        def act(zz):
            if do is start:
                arrival(0, place.b_first, zz)
            for copy in transfers(1, place.b_first, zz, 3, (0, place.b_first_of_second), place.second):
                do(copy)
            for copy in to_siblings(1, place.b_first, zz):
                do(copy)

        when(entry, act)

    def second_stage(entry, do):
        def act(zz):
            if do is start:
                arrival(0, place.b_second, zz)
            for copy in to_siblings(1, place.b_second, zz):
                do(copy)

        when(entry, act)

    def edges(do):
        for step in range(1, nz):
            device = place.along_z(step)
            for q, (own, grid) in enumerate(edge_pairs):
                do(remote(own.at[device[2]], grid.at[z], e_send.at[q, step],
                          e_receive.at[q, step], device))

    def start(copy):
        copy.start()

    def finish(copy):
        copy.wait_send()

    place.b_first_of_second = place.b_second
    rounds = [[(0, 0)]] + [[(s, -1), (s, 1)] for s in range(1, nz)]
    for r in range(nz + 2):
        if r < nz:
            for entry in rounds[r]:
                own_stage(entry, start)
        if r == 0:
            edges(start)
        if 1 <= r <= nz:
            for entry in rounds[r - 1]:
                first_stage(entry, start)
        if r >= 2:
            for entry in rounds[r - 2]:
                second_stage(entry, start)

    for copy in locals_:
        copy.wait()
    for entry in entries:
        own_stage(entry, finish)
        first_stage(entry, finish)
        second_stage(entry, finish)
    edges(lambda copy: copy.wait())
    for a in range(1, 1 + len(place.siblings)):
        for b in range(3):
            for zz in range(nz):
                arrival(a, b, zz)


def edge_kernel(nz, halo, g_ref, hg_ref, bg_ref, mg_ref, w1_ref, w2_ref, out_ref, table, w_mix):
    na = g_ref.shape[0]
    atoms, width = g_ref.shape[3:]
    slots = mg_ref.shape[2]
    radial = bg_ref.shape[2]
    lanes = hg_ref.shape[4]
    group = na * 3 * halo
    w_mix[:radial, :] = w1_ref[2 * width :, :]
    rest = table.shape[0] - (nz + 2) * group
    table[(nz + 2) * group :, :] = jnp.zeros((rest, width), jnp.bfloat16)
    lane = lax.broadcasted_iota(jnp.int32, (lanes, lanes), 1).astype(jnp.float32)

    def fill(z, carry):
        for a in range(na):
            for b in range(3):
                index = jnp.broadcast_to(hg_ref[a, b, z, 0:1, :], (lanes, lanes)).T
                pick = (index == lane).astype(jnp.bfloat16)[:halo, :atoms]
                rows = jnp.dot(pick, g_ref[a, b, z], preferred_element_type=jnp.float32).astype(jnp.bfloat16)
                at = (a * 3 + b) * halo
                table[pl.ds(pl.multiple_of((z + 1) * group + at, 16), halo), :] = rows

                @pl.when(z == 0)
                def _():
                    table[pl.ds((nz + 1) * group + at, halo), :] = rows

                @pl.when(z == nz - 1)
                def _():
                    table[pl.ds(at, halo), :] = rows
        return carry

    lax.fori_loop(0, nz, fill, 0)
    window = -(-3 * group // lanes) * lanes
    lane_s = lax.broadcasted_iota(jnp.int32, (slots, lanes), 1).astype(jnp.float32)
    sublane = lax.broadcasted_iota(jnp.int32, (atoms, slots), 0).astype(jnp.float32)

    def domain(o, carry):
        position = jnp.broadcast_to(mg_ref[o, 0:1, :], (lanes, slots)).T
        target = jnp.broadcast_to(mg_ref[o, 1:2, :], (lanes, slots)).T
        own = g_ref[0, 1, o]
        pick = (position == lane_s).astype(jnp.bfloat16)
        source = jnp.dot(pick, own, preferred_element_type=jnp.float32)
        picks = jnp.concatenate(
            [(position - float(atoms + j * lanes) == lane_s).astype(jnp.bfloat16) for j in range(window // lanes)],
            axis=1,
        )
        rows = table[pl.ds(pl.multiple_of(o * group, 16), window), :]
        source = source + jnp.dot(picks, rows, preferred_element_type=jnp.float32)
        w_mix[radial:, :] = jnp.dot(
            own, w1_ref[width : 2 * width, :], preferred_element_type=jnp.float32
        ).astype(jnp.bfloat16)
        mix = jnp.concatenate([bg_ref[o], (target == lane_s).astype(jnp.bfloat16)], axis=1)
        pre = jnp.dot(source.astype(jnp.bfloat16), w1_ref[:width, :], preferred_element_type=jnp.float32)
        pre = pre + jnp.dot(mix, w_mix[...], preferred_element_type=jnp.float32)
        half = 0.5 * pre
        hidden = (half + half * jnp.tanh(half)).astype(jnp.bfloat16)
        incidence = (jnp.broadcast_to(mg_ref[o, 1:2, :], (atoms, slots)) == sublane).astype(jnp.bfloat16)
        summed = jnp.dot(incidence, hidden, preferred_element_type=jnp.float32).astype(jnp.bfloat16)
        out_ref[o] = jnp.dot(summed, w2_ref[...], preferred_element_type=jnp.float32).astype(jnp.bfloat16)
        return carry

    lax.fori_loop(0, nz, domain, 0)


def update_kernel(sizes, halo, part_ref, f_ref, h_ref, w_ref, new_ref, n_ref,
                  landed, edge_rows, p_send, p_receive, send, receive, local):
    place = Place(sizes)
    z, nz = place.z, place.nz
    place.meet()
    copies = []
    for step in range(1, nz):
        device = place.along_z(step)
        copies.append(remote(part_ref.at[device[2]], landed.at[step - 1], p_send.at[step],
                             p_receive.at[step], device))
    for copy in copies:
        copy.start()
    total = part_ref[z].astype(jnp.float32)
    for step, copy in enumerate(copies):
        copy.wait_recv()
        total = total + landed[step].astype(jnp.float32)
    mean_square = jnp.mean(total * total, axis=-1, keepdims=True)
    normed = (total * lax.rsqrt(mean_square + 1e-05)).astype(jnp.bfloat16)
    update = jnp.dot(normed, w_ref[...], preferred_element_type=jnp.float32)
    new_rows = (f_ref[...].astype(jnp.float32) + update).astype(jnp.bfloat16)
    lanes = h_ref.shape[1]
    atoms = f_ref.shape[0]
    lane = lax.broadcasted_iota(jnp.int32, (lanes, lanes), 1).astype(jnp.float32)
    index = jnp.broadcast_to(h_ref[0:1, :], (lanes, lanes)).T
    pick = (index == lane).astype(jnp.bfloat16)[:halo, :atoms]
    edge_rows[...] = jnp.dot(pick, new_rows, preferred_element_type=jnp.float32).astype(jnp.bfloat16)
    new_ref[...] = new_rows

    started = []

    def begin(b, c, kind, slot, device):
        source = edge_rows if (b is None and c == 1) else n_ref.at[0, 1 if b is None else b, c]
        index = 1 if b is None else b
        copy = remote(source, n_ref.at[slot], send.at[kind, index, c], receive.at[slot], device)
        copy.start()
        started.append(copy)

    def arrival(a, b, c):
        remote(n_ref.at[a, b, c], n_ref.at[a, b, c], send.at[0, 0, 0], receive.at[a, b, c], place.first).wait_recv()

    def to_siblings(b, c):
        for i, device in enumerate(place.siblings):
            begin(b, c, 3 + i, (place.sibling_slot(i), 1 if b is None else b, c), device)

    begin(None, 1, 0, (0, 1, 0), place.along_z(1))
    begin(None, 1, 1, (0, 1, 2), place.along_z(-1))
    begin(None, 1, 2, (0, 2 - place.b_first, 1), place.first)
    to_siblings(None, 1)
    own = pltpu.make_async_copy(edge_rows, n_ref.at[0, 1, 1], local)
    own.start()
    order = (1, 0, 2)
    for c in order[1:]:
        arrival(0, 1, c)
        begin(None, c, 2, (0, 2 - place.b_first, c), place.first)
        to_siblings(None, c)
    for c in order:
        arrival(0, place.b_first, c)
        begin(place.b_first, c, 2, (0, place.b_second, c), place.second)
        to_siblings(place.b_first, c)
    for c in order:
        arrival(0, place.b_second, c)
        to_siblings(place.b_second, c)
    for a in range(1, 1 + len(place.siblings)):
        for b in range(3):
            for c in range(3):
                arrival(a, b, c)
    own.wait()
    for copy in copies + started:
        copy.wait_send()


def slots_of(nx):
    return (1, 0, 1) if nx == 2 else (2, 0, 1)


def shards(sizes, features, halo_index, edge_src, edge_dst, edge_count, edge_basis, w_edge_in, w_edge_out, w_update):
    nx, ny, nz = sizes
    atoms, width = features.shape
    groups, slots = edge_src.shape
    halo = halo_index.shape[0]
    radial = edge_basis.shape[1]
    hidden = w_edge_in.shape[2]
    lanes = -(-max(atoms, halo) // 128) * 128
    na = 2 if nx == 2 else 3
    f32, bf16 = jnp.float32, jnp.bfloat16

    index = jnp.pad(halo_index.astype(f32)[None, :], ((0, 7), (0, lanes - halo)), constant_values=-1.0)
    beyond = edge_src - atoms
    offset = beyond // halo
    offset = offset + (offset >= 13)
    off_x, off_y, off_z = offset // 9, (offset // 3) % 3, offset % 3
    slot_x = jnp.where(off_x == 1, 0, jnp.where(off_x == 2, 1, na - 1))
    position = atoms + ((off_z * na + slot_x) * 3 + off_y) * halo + beyond % halo
    position = jnp.where(edge_src < atoms, edge_src, position)
    live = lax.broadcasted_iota(jnp.int32, (groups, slots), 1) < edge_count[:, None]
    target = jnp.where(live, edge_dst, -1)
    meta = jnp.stack([position, target], axis=1).astype(f32)
    meta = jnp.pad(meta, ((0, 0), (0, 6), (0, 0)))
    basis = edge_basis.reshape(groups, slots, radial)

    vmem = pl.BlockSpec(memory_space=pltpu.VMEM)
    anywhere = pl.BlockSpec(memory_space=pl.ANY)
    dma = pltpu.SemaphoreType.DMA
    kinds = 4 + (na - 1)
    grid, index_grid, basis_all, meta_all = pl.pallas_call(
        functools.partial(gather_kernel, sizes),
        out_shape=(
            jax.ShapeDtypeStruct((na, 3, nz, atoms, width), bf16),
            jax.ShapeDtypeStruct((na, 3, nz, 8, lanes), f32),
            jax.ShapeDtypeStruct((nz, slots, radial), bf16),
            jax.ShapeDtypeStruct((nz, 8, slots), f32),
        ),
        in_specs=[anywhere] * 4,
        out_specs=(anywhere,) * 4,
        scratch_shapes=[
            dma((2, kinds, 3, nz)),
            dma((2, na, 3, nz)),
            dma((2, nz)),
            dma((2, nz)),
            dma((4,)),
        ],
        compiler_params=pltpu.CompilerParams(collective_id=0, has_side_effects=True),
        name="gather_blocks",
    )(features, index, basis, meta)

    group = na * 3 * halo
    window = -(-3 * group // lanes) * lanes
    table_rows = (nz - 1) * group + window
    partial_sums = pl.pallas_call(
        functools.partial(edge_kernel, nz, halo),
        out_shape=jax.ShapeDtypeStruct((nz, atoms, width), bf16),
        in_specs=[vmem] * 6,
        out_specs=vmem,
        scratch_shapes=[
            pltpu.VMEM((table_rows, width), bf16),
            pltpu.VMEM((radial + lanes, hidden), bf16),
        ],
        compiler_params=pltpu.CompilerParams(vmem_limit_bytes=60 * 1024 * 1024),
        name="edge_network",
    )(grid, index_grid, basis_all, meta_all, w_edge_in[0], w_edge_out[0])

    new_rows, blocks = pl.pallas_call(
        functools.partial(update_kernel, sizes, halo),
        out_shape=(
            jax.ShapeDtypeStruct((atoms, width), bf16),
            jax.ShapeDtypeStruct((na, 3, 3, halo, width), bf16),
        ),
        in_specs=[vmem] * 4,
        out_specs=(vmem, anywhere),
        scratch_shapes=[
            pltpu.VMEM((nz - 1, atoms, width), bf16),
            pltpu.VMEM((halo, width), bf16),
            dma((nz,)),
            dma((nz,)),
            dma((3 + na - 1, 3, 3)),
            dma((na, 3, 3)),
            dma(()),
        ],
        compiler_params=pltpu.CompilerParams(collective_id=1, has_side_effects=True),
        name="update_blocks",
    )(partial_sums, features, index, w_update)

    slot = slots_of(nx)
    chosen = [
        blocks[slot[a], b, c]
        for a in range(3)
        for b in range(3)
        for c in range(3)
        if (a, b, c) != (1, 1, 1)
    ]
    return new_rows, jnp.stack(chosen)


def solution(mesh):
    sizes = tuple(mesh.shape[name] for name in AXES)
    in_specs = (
        P(AXES, None),
        P(AXES),
        P(AXES, None),
        P(AXES, None),
        P(AXES),
        P(AXES, None),
        P("gz", None, None),
        P("gz", None, None),
        P(),
    )
    out_specs = (P(AXES, None), P(AXES, None, None))
    return jax.shard_map(
        functools.partial(shards, sizes), mesh=mesh, in_specs=in_specs, out_specs=out_specs, check_vma=False
    )
```

```python
import functools

import jax
import jax.numpy as jnp
from jax import lax
from jax.experimental import pallas as pl
from jax.experimental.pallas import tpu as pltpu
from jax.sharding import PartitionSpec as P

AXES = ("gx", "gy", "gz")
MESH = pl.DeviceIdType.MESH


class Place:
    def __init__(self, sizes):
        self.nx, self.ny, self.nz = sizes
        self.x, self.y, self.z = (lax.axis_index(name) for name in AXES)
        x, y, z = self.x, self.y, self.z
        self.first = (x, y + 1 - 2 * lax.rem(y, 2), z)
        self.second = (x, lax.rem(y + 2, 4), z)
        self.b_first = 2 - 2 * lax.rem(y, 2)
        self.b_second = 2 * lax.rem(y, 2)
        self.siblings = [(lax.rem(x + 1, self.nx), y, z)]
        if self.nx > 2:
            self.siblings.append((lax.rem(x + self.nx - 1, self.nx), y, z))

    def along_z(self, step):
        return (self.x, self.y, lax.rem(self.z + step + self.nz, self.nz))

    def sibling_slot(self, index):
        return 1 if self.nx == 2 else 2 - index

    def meet(self):
        barrier = pltpu.get_barrier_semaphore()
        partners = [self.along_z(step) for step in range(1, self.nz)]
        partners += [self.first, self.second] + self.siblings
        for partner in partners:
            pl.semaphore_signal(barrier, inc=1, device_id=partner, device_id_type=MESH)
        pl.semaphore_wait(barrier, len(partners))


def remote(source, target, send, receive, device):
    return pltpu.make_async_remote_copy(
        src_ref=source,
        dst_ref=target,
        send_sem=send,
        recv_sem=receive,
        device_id=device,
        device_id_type=MESH,
    )


def layer_kernel(sizes, f_ref, index_ref, src_ref, dst_ref, count_ref, basis_ref, w1_hbm, w2_hbm, w3_hbm,
                 new_ref, out_ref,
                 h_ref, meta_ref, g_ref, hg_ref, bg_ref, mg_ref, w1_ref, w2_ref, w3_ref, table, w_mix,
                 part_ref, landed, edge_rows, n_ref,
                 send, receive, e_send, e_receive, local, p_send, p_receive, n_send, n_receive, o_sem):
    place = Place(sizes)
    z, nz = place.z, place.nz
    halo = index_ref.shape[1]
    na = g_ref.shape[0]
    atoms, width = g_ref.shape[3:]
    groups, slots = src_ref.shape
    radial = bg_ref.shape[2]
    lanes = hg_ref.shape[4]
    group = na * 3 * halo
    f32, bf16 = jnp.float32, jnp.bfloat16
    pairs = ((f_ref, g_ref), (h_ref, hg_ref))
    edge_pairs = ((meta_ref, mg_ref), (basis_ref, bg_ref))

    weights = [
        pltpu.make_async_copy(w1_hbm, w1_ref, local.at[0]),
        pltpu.make_async_copy(w2_hbm, w2_ref, local.at[1]),
        pltpu.make_async_copy(w3_hbm, w3_ref, local.at[2]),
    ]
    own_basis = pltpu.make_async_copy(basis_ref.at[z], bg_ref.at[z], local.at[3])
    for copy in weights + [own_basis]:
        copy.start()

    h_ref[...] = jnp.full(h_ref.shape, -1.0, f32)
    h_ref[0:1, :halo] = index_ref[...].astype(f32)
    edge_src = src_ref[...].astype(f32)
    beyond = edge_src - float(atoms)
    offset = jnp.floor((beyond + 0.5) * (1.0 / halo))
    slot = beyond - offset * float(halo)
    offset = jnp.where(offset >= 13.0, offset + 1.0, offset)
    off_x = jnp.floor((offset + 0.5) * (1.0 / 9.0))
    inner = offset - 9.0 * off_x
    off_y = jnp.floor((inner + 0.5) * (1.0 / 3.0))
    off_z = inner - 3.0 * off_y
    slot_x = jnp.where(off_x == 1.0, 0.0, jnp.where(off_x == 2.0, 1.0, float(na - 1)))
    position = float(atoms) + ((off_z * float(na) + slot_x) * 3.0 + off_y) * float(halo) + slot
    position = jnp.where(edge_src < float(atoms), edge_src, position)
    row_lane = lax.broadcasted_iota(jnp.int32, (1, slots), 1)
    meta_ref[...] = jnp.zeros_like(meta_ref)
    for j in range(groups):
        meta_ref[j, 0:1, :] = position[j : j + 1, :]
        target = jnp.where(row_lane < count_ref[j], dst_ref[j : j + 1, :], -1)
        meta_ref[j, 1:2, :] = target.astype(f32)
    g_ref[0, 1, z] = f_ref[...]
    hg_ref[0, 1, z] = h_ref[...]
    mg_ref[z] = meta_ref[z]
    place.meet()

    def when(entry, action):
        s, sign = entry
        zz = z + sign * s
        if s == 0:
            action(zz)
        else:
            pl.when((zz >= 0) & (zz < nz))(functools.partial(action, zz))

    def transfers(s, b, zz, kind, slot, device):
        out = []
        for q, (own, grid) in enumerate(pairs):
            index = 1 if b is None else b
            source = own if (s == 0 and b is None) else grid.at[0, index, zz]
            out.append(remote(source, grid.at[slot[0], slot[1], zz], send.at[q, kind, index, zz],
                              receive.at[q, slot[0], slot[1], zz], device))
        return out

    def to_siblings(s, b, zz):
        out = []
        for i, device in enumerate(place.siblings):
            slot = (place.sibling_slot(i), 1 if b is None else b)
            out += transfers(s, b, zz, 4 + i, slot, device)
        return out

    def arrival(a, b, zz):
        for q, (own, grid) in enumerate(pairs):
            remote(grid.at[a, b, zz], grid.at[a, b, zz], send.at[q, 0, 0, 0],
                   receive.at[q, a, b, zz], place.first).wait_recv()

    def chain(entry, zz, do):
        s, sign = entry
        if s < nz - 1:
            for go in ((1, -1) if s == 0 else (-sign,)):
                device = (place.x, place.y, z + go)

                def act():
                    for copy in transfers(s, None, zz, 0 if go > 0 else 1, (0, 1), device):
                        do(copy)

                pl.when((z + go >= 0) & (z + go < nz))(act)

    def own_stage(entry, do):
        def act(zz):
            if entry[0] > 0 and do is start:
                arrival(0, 1, zz)
            chain(entry, zz, do)
            for copy in transfers(entry[0], None, zz, 2, (0, place.b_second), place.first):
                do(copy)
            for copy in to_siblings(entry[0], None, zz):
                do(copy)

        when(entry, act)

    def first_stage(entry, do):
        def act(zz):
            if do is start:
                arrival(0, place.b_first, zz)
            for copy in transfers(1, place.b_first, zz, 3, (0, place.b_second), place.second):
                do(copy)
            for copy in to_siblings(1, place.b_first, zz):
                do(copy)

        when(entry, act)

    def second_stage(entry, do):
        def act(zz):
            if do is start:
                arrival(0, place.b_second, zz)
            for copy in to_siblings(1, place.b_second, zz):
                do(copy)

        when(entry, act)

    def edges(q, do):
        own, grid = edge_pairs[q]
        for step in range(1, nz):
            device = place.along_z(step)
            do(remote(own.at[device[2]], grid.at[z], e_send.at[q, step], e_receive.at[q, step], device))

    def start(copy):
        copy.start()

    def finish(copy):
        copy.wait_send()

    rounds = [[(0, 0)]] + [[(s, -1), (s, 1)] for s in range(1, nz)]
    for r in range(nz + 2):
        if r < nz:
            for entry in rounds[r]:
                own_stage(entry, start)
        if r == 0:
            edges(0, start)
        if r == nz - 1:
            edges(1, start)
        if 1 <= r <= nz:
            for entry in rounds[r - 1]:
                first_stage(entry, start)
        if r >= 2:
            for entry in rounds[r - 2]:
                second_stage(entry, start)
    for copy in weights + [own_basis]:
        copy.wait()
    w_mix[:radial, :] = w1_ref[2 * width :, :]
    rest = table.shape[0] - (nz + 2) * group
    table[(nz + 2) * group :, :] = jnp.zeros((rest, width), bf16)
    for a in range(1, na):
        for b in range(3):
            for zz in range(nz):
                arrival(a, b, zz)
    edges(0, lambda copy: copy.wait_recv())
    edges(1, lambda copy: copy.wait_recv())

    lane = lax.broadcasted_iota(jnp.int32, (lanes, lanes), 1).astype(f32)

    def boundary(index_row, rows):
        index = jnp.broadcast_to(index_row, (lanes, lanes)).T
        pick = (index == lane).astype(bf16)[:halo, :atoms]
        return jnp.dot(pick, rows, preferred_element_type=f32).astype(bf16)

    def fill(zz, carry):
        for a in range(na):
            for b in range(3):
                rows = boundary(hg_ref[a, b, zz, 0:1, :], g_ref[a, b, zz])
                at = (a * 3 + b) * halo
                table[pl.ds(pl.multiple_of((zz + 1) * group + at, 16), halo), :] = rows

                @pl.when(zz == 0)
                def _():
                    table[pl.ds((nz + 1) * group + at, halo), :] = rows

                @pl.when(zz == nz - 1)
                def _():
                    table[pl.ds(at, halo), :] = rows
        return carry

    lax.fori_loop(0, nz, fill, 0)
    window = -(-3 * group // lanes) * lanes
    lane_s = lax.broadcasted_iota(jnp.int32, (slots, lanes), 1).astype(f32)
    sublane = lax.broadcasted_iota(jnp.int32, (atoms, slots), 0).astype(f32)

    def domain(o):
        position = jnp.broadcast_to(mg_ref[o, 0:1, :], (lanes, slots)).T
        target = jnp.broadcast_to(mg_ref[o, 1:2, :], (lanes, slots)).T
        own = g_ref[0, 1, o]
        pick = (position == lane_s).astype(bf16)
        source = jnp.dot(pick, own, preferred_element_type=f32)
        picks = jnp.concatenate(
            [(position - float(atoms + j * lanes) == lane_s).astype(bf16) for j in range(window // lanes)],
            axis=1,
        )
        rows = table[pl.ds(pl.multiple_of(o * group, 16), window), :]
        source = source + jnp.dot(picks, rows, preferred_element_type=f32)
        w_mix[radial:, :] = jnp.dot(
            own, w1_ref[width : 2 * width, :], preferred_element_type=f32
        ).astype(bf16)
        mix = jnp.concatenate([bg_ref[o], (target == lane_s).astype(bf16)], axis=1)
        pre = jnp.dot(source.astype(bf16), w1_ref[:width, :], preferred_element_type=f32)
        pre = pre + jnp.dot(mix, w_mix[...], preferred_element_type=f32)
        half = 0.5 * pre
        hidden = (half + half * jnp.tanh(half)).astype(bf16)
        incidence = (jnp.broadcast_to(mg_ref[o, 1:2, :], (atoms, slots)) == sublane).astype(bf16)
        summed = jnp.dot(incidence, hidden, preferred_element_type=f32).astype(bf16)
        return jnp.dot(summed, w2_ref[...], preferred_element_type=f32)

    def returned(step):
        device = place.along_z(step + 1)
        return remote(part_ref.at[step], landed.at[step], p_send.at[step], p_receive.at[step], device)

    def other(step, carry):
        part_ref[step] = domain(lax.rem(z + step + 1, nz)).astype(bf16)
        returned(step).start()
        return carry

    lax.fori_loop(0, nz - 1, other, 0)
    total = domain(z)
    for step in range(nz - 1):
        returned(step).wait_recv()
        total = total + landed[step].astype(f32)
    mean_square = jnp.mean(total * total, axis=-1, keepdims=True)
    normed = (total * lax.rsqrt(mean_square + 1e-05)).astype(bf16)
    update = jnp.dot(normed, w3_ref[...], preferred_element_type=f32)
    new_rows = (f_ref[...].astype(f32) + update).astype(bf16)
    edge_rows[...] = boundary(h_ref[0:1, :], new_rows)
    new_ref[...] = new_rows

    started = []
    written = []

    def begin(b, c, kind, slot, device):
        source = edge_rows if (b is None and c == 1) else n_ref.at[0, 1 if b is None else b, c]
        index = 1 if b is None else b
        copy = remote(source, n_ref.at[slot], n_send.at[kind, index, c], n_receive.at[slot], device)
        copy.start()
        started.append(copy)

    def landing(a, b, c):
        remote(n_ref.at[a, b, c], n_ref.at[a, b, c], n_send.at[0, 0, 0], n_receive.at[a, b, c], place.first).wait_recv()

    def write(a, b, c):
        for part, slot in enumerate((1, 0, 1) if na == 2 else (2, 0, 1)):
            if slot == a:
                cell = part * 9 + b * 3 + c
                cell = cell - 1 if isinstance(cell, int) and cell > 13 else cell
                if not isinstance(cell, int):
                    cell = jnp.where(cell > 13, cell - 1, cell)
                copy = pltpu.make_async_copy(n_ref.at[a, b, c], out_ref.at[cell], o_sem.at[cell])
                copy.start()
                written.append(copy)

    def to_siblings_next(b, c):
        for i, device in enumerate(place.siblings):
            begin(b, c, 3 + i, (place.sibling_slot(i), 1 if b is None else b, c), device)

    begin(None, 1, 0, (0, 1, 0), place.along_z(1))
    begin(None, 1, 1, (0, 1, 2), place.along_z(-1))
    begin(None, 1, 2, (0, place.b_second, 1), place.first)
    to_siblings_next(None, 1)
    order = (1, 0, 2)
    for c in order[1:]:
        landing(0, 1, c)
        begin(None, c, 2, (0, place.b_second, c), place.first)
        to_siblings_next(None, c)
        write(0, 1, c)
    for c in order:
        landing(0, place.b_first, c)
        begin(place.b_first, c, 2, (0, place.b_second, c), place.second)
        to_siblings_next(place.b_first, c)
        write(0, place.b_first, c)
    for c in order:
        landing(0, place.b_second, c)
        to_siblings_next(place.b_second, c)
        write(0, place.b_second, c)
    for b in (1, place.b_first, place.b_second):
        for a in range(1, na):
            for c in order:
                landing(a, b, c)
                write(a, b, c)
    for group_ in rounds:
        for entry in group_:
            own_stage(entry, finish)
            first_stage(entry, finish)
            second_stage(entry, finish)
    for q in range(2):
        edges(q, finish)
    for step in range(nz - 1):
        returned(step).wait_send()
    for copy in started:
        copy.wait_send()
    for copy in written:
        copy.wait()


def shards(sizes, features, halo_index, edge_src, edge_dst, edge_count, edge_basis, w_edge_in, w_edge_out, w_update):
    nx, ny, nz = sizes
    atoms, width = features.shape
    groups, slots = edge_src.shape
    halo = halo_index.shape[0]
    radial = edge_basis.shape[1]
    hidden = w_edge_in.shape[2]
    lanes = -(-max(atoms, halo) // 128) * 128
    na = 2 if nx == 2 else 3
    f32, bf16 = jnp.float32, jnp.bfloat16
    basis = edge_basis.reshape(groups, slots, radial)
    vmem = pl.BlockSpec(memory_space=pltpu.VMEM)
    smem = pl.BlockSpec(memory_space=pltpu.SMEM)
    anywhere = pl.BlockSpec(memory_space=pl.ANY)
    dma = pltpu.SemaphoreType.DMA
    kinds = 4 + (na - 1)
    group = na * 3 * halo
    window = -(-3 * group // lanes) * lanes
    table_rows = (nz - 1) * group + window
    new_rows, blocks = pl.pallas_call(
        functools.partial(layer_kernel, sizes),
        out_shape=(
            jax.ShapeDtypeStruct((atoms, width), bf16),
            jax.ShapeDtypeStruct((26, halo, width), bf16),
        ),
        in_specs=[vmem, vmem, vmem, vmem, smem, anywhere, anywhere, anywhere, anywhere],
        out_specs=(vmem, anywhere),
        scratch_shapes=[
            pltpu.VMEM((8, lanes), f32),
            pltpu.VMEM((nz, 8, slots), f32),
            pltpu.VMEM((na, 3, nz, atoms, width), bf16),
            pltpu.VMEM((na, 3, nz, 8, lanes), f32),
            pltpu.VMEM((nz, slots, radial), bf16),
            pltpu.VMEM((nz, 8, slots), f32),
            pltpu.VMEM(w_edge_in.shape[1:], bf16),
            pltpu.VMEM(w_edge_out.shape[1:], bf16),
            pltpu.VMEM(w_update.shape, bf16),
            pltpu.VMEM((table_rows, width), bf16),
            pltpu.VMEM((radial + lanes, hidden), bf16),
            pltpu.VMEM((nz - 1, atoms, width), bf16),
            pltpu.VMEM((nz - 1, atoms, width), bf16),
            pltpu.VMEM((halo, width), bf16),
            pltpu.VMEM((na, 3, 3, halo, width), bf16),
            dma((2, kinds, 3, nz)),
            dma((2, na, 3, nz)),
            dma((2, nz)),
            dma((2, nz)),
            dma((4,)),
            dma((nz - 1,)),
            dma((nz - 1,)),
            dma((3 + na - 1, 3, 3)),
            dma((na, 3, 3)),
            dma((26,)),
        ],
        compiler_params=pltpu.CompilerParams(
            collective_id=0, has_side_effects=True, vmem_limit_bytes=60 * 1024 * 1024
        ),
        name="layer",
    )(features, halo_index.reshape(1, halo), edge_src, edge_dst, edge_count, basis,
      w_edge_in[0], w_edge_out[0], w_update)
    return new_rows, blocks


def solution(mesh):
    sizes = tuple(mesh.shape[name] for name in AXES)
    in_specs = (
        P(AXES, None),
        P(AXES),
        P(AXES, None),
        P(AXES, None),
        P(AXES),
        P(AXES, None),
        P("gz", None, None),
        P("gz", None, None),
        P(),
    )
    out_specs = (P(AXES, None), P(AXES, None, None))
    return jax.shard_map(
        functools.partial(shards, sizes), mesh=mesh, in_specs=in_specs, out_specs=out_specs, check_vma=False
    )
```

```python
import functools

import jax
import jax.numpy as jnp
from jax import lax
from jax.experimental import pallas as pl
from jax.experimental.pallas import tpu as pltpu
from jax.sharding import PartitionSpec as P

AXES = ("gx", "gy", "gz")
MESH = pl.DeviceIdType.MESH


class Place:
    def __init__(self, sizes):
        self.nx, self.ny, self.nz = sizes
        self.x, self.y, self.z = (lax.axis_index(name) for name in AXES)
        x, y, z = self.x, self.y, self.z
        self.first = (x, y + 1 - 2 * lax.rem(y, 2), z)
        self.second = (x, lax.rem(y + 2, 4), z)
        self.b_first = 2 - 2 * lax.rem(y, 2)
        self.b_second = 2 * lax.rem(y, 2)
        self.siblings = [(lax.rem(x + 1, self.nx), y, z)]
        if self.nx > 2:
            self.siblings.append((lax.rem(x + self.nx - 1, self.nx), y, z))

    def along_z(self, step):
        return (self.x, self.y, lax.rem(self.z + step + self.nz, self.nz))

    def sibling_slot(self, index):
        return 1 if self.nx == 2 else 2 - index

    def meet(self):
        barrier = pltpu.get_barrier_semaphore()
        partners = [self.along_z(step) for step in range(1, self.nz)]
        partners += [self.first, self.second] + self.siblings
        for partner in partners:
            pl.semaphore_signal(barrier, inc=1, device_id=partner, device_id_type=MESH)
        pl.semaphore_wait(barrier, len(partners))


def remote(source, target, send, receive, device):
    return pltpu.make_async_remote_copy(
        src_ref=source,
        dst_ref=target,
        send_sem=send,
        recv_sem=receive,
        device_id=device,
        device_id_type=MESH,
    )


def layer_kernel(sizes, f_ref, index_ref, src_ref, dst_ref, count_ref, basis_ref, w1_hbm, w2_hbm, w3_hbm,
                 new_ref, out_ref,
                 h_ref, meta_ref, g_ref, hg_ref, bg_ref, mg_ref, w1_ref, w2_ref, w3_ref, table, w_mix,
                 part_ref, landed, edge_rows, fresh, n_ref,
                 send, receive, e_send, e_receive, local, p_send, p_receive, n_send, n_receive, o_sem):
    place = Place(sizes)
    z, nz = place.z, place.nz
    halo = index_ref.shape[1]
    na = g_ref.shape[0]
    atoms, width = g_ref.shape[3:]
    groups, slots = src_ref.shape
    radial = bg_ref.shape[2]
    lanes = hg_ref.shape[4]
    group = na * 3 * halo
    f32, bf16 = jnp.float32, jnp.bfloat16
    pairs = ((f_ref, g_ref), (h_ref, hg_ref))
    edge_pairs = ((meta_ref, mg_ref), (basis_ref, bg_ref))

    weights = [
        pltpu.make_async_copy(w1_hbm, w1_ref, local.at[0]),
        pltpu.make_async_copy(w2_hbm, w2_ref, local.at[1]),
        pltpu.make_async_copy(w3_hbm, w3_ref, local.at[2]),
    ]
    own_basis = pltpu.make_async_copy(basis_ref.at[z], bg_ref.at[z], local.at[3])
    for copy in weights + [own_basis]:
        copy.start()

    h_ref[...] = jnp.full(h_ref.shape, -1.0, f32)
    h_ref[0:1, :halo] = index_ref[...].astype(f32)
    edge_src = src_ref[...].astype(f32)
    beyond = edge_src - float(atoms)
    offset = jnp.floor((beyond + 0.5) * (1.0 / halo))
    slot = beyond - offset * float(halo)
    offset = jnp.where(offset >= 13.0, offset + 1.0, offset)
    off_x = jnp.floor((offset + 0.5) * (1.0 / 9.0))
    inner = offset - 9.0 * off_x
    off_y = jnp.floor((inner + 0.5) * (1.0 / 3.0))
    off_z = inner - 3.0 * off_y
    slot_x = jnp.where(off_x == 1.0, 0.0, jnp.where(off_x == 2.0, 1.0, float(na - 1)))
    position = float(atoms) + ((off_z * float(na) + slot_x) * 3.0 + off_y) * float(halo) + slot
    position = jnp.where(edge_src < float(atoms), edge_src, position)
    row_lane = lax.broadcasted_iota(jnp.int32, (1, slots), 1)
    meta_ref[...] = jnp.zeros_like(meta_ref)
    for j in range(groups):
        meta_ref[j, 0:1, :] = position[j : j + 1, :]
        target = jnp.where(row_lane < count_ref[j], dst_ref[j : j + 1, :], -1)
        meta_ref[j, 1:2, :] = target.astype(f32)
    g_ref[0, 1, z] = f_ref[...]
    hg_ref[0, 1, z] = h_ref[...]
    mg_ref[z] = meta_ref[z]
    place.meet()

    def when(entry, action):
        s, sign = entry
        zz = z + sign * s
        if s == 0:
            action(zz)
        else:
            pl.when((zz >= 0) & (zz < nz))(functools.partial(action, zz))

    def transfers(s, b, zz, kind, slot, device):
        out = []
        for q, (own, grid) in enumerate(pairs):
            index = 1 if b is None else b
            source = own if (s == 0 and b is None) else grid.at[0, index, zz]
            out.append(remote(source, grid.at[slot[0], slot[1], zz], send.at[q, kind, index, zz],
                              receive.at[q, slot[0], slot[1], zz], device))
        return out

    def to_siblings(s, b, zz):
        out = []
        for i, device in enumerate(place.siblings):
            slot = (place.sibling_slot(i), 1 if b is None else b)
            out += transfers(s, b, zz, 4 + i, slot, device)
        return out

    def arrival(a, b, zz):
        for q, (own, grid) in enumerate(pairs):
            remote(grid.at[a, b, zz], grid.at[a, b, zz], send.at[q, 0, 0, 0],
                   receive.at[q, a, b, zz], place.first).wait_recv()

    def chain(entry, zz, do):
        s, sign = entry
        if s < nz - 1:
            for go in ((1, -1) if s == 0 else (-sign,)):
                device = (place.x, place.y, z + go)

                def act():
                    for copy in transfers(s, None, zz, 0 if go > 0 else 1, (0, 1), device):
                        do(copy)

                pl.when((z + go >= 0) & (z + go < nz))(act)

    def own_stage(entry, do):
        def act(zz):
            if entry[0] > 0 and do is start:
                arrival(0, 1, zz)
            chain(entry, zz, do)
            for copy in transfers(entry[0], None, zz, 2, (0, place.b_second), place.first):
                do(copy)
            for copy in to_siblings(entry[0], None, zz):
                do(copy)

        when(entry, act)

    def first_stage(entry, do):
        def act(zz):
            if do is start:
                arrival(0, place.b_first, zz)
            for copy in transfers(1, place.b_first, zz, 3, (0, place.b_second), place.second):
                do(copy)
            for copy in to_siblings(1, place.b_first, zz):
                do(copy)

        when(entry, act)

    def second_stage(entry, do):
        def act(zz):
            if do is start:
                arrival(0, place.b_second, zz)
            for copy in to_siblings(1, place.b_second, zz):
                do(copy)

        when(entry, act)

    def edges(q, do):
        own, grid = edge_pairs[q]
        for step in range(1, nz):
            device = place.along_z(step)
            do(remote(own.at[device[2]], grid.at[z], e_send.at[q, step], e_receive.at[q, step], device))

    def start(copy):
        copy.start()

    def finish(copy):
        copy.wait_send()

    lane = lax.broadcasted_iota(jnp.int32, (lanes, lanes), 1).astype(f32)

    def boundary(index_row, rows):
        index = jnp.broadcast_to(index_row, (lanes, lanes)).T
        pick = (index == lane).astype(bf16)[:halo, :atoms]
        return jnp.dot(pick, rows, preferred_element_type=f32).astype(bf16)

    def fill(a, b, zz):
        rows = boundary(hg_ref[a, b, zz, 0:1, :], g_ref[a, b, zz])
        at = pl.multiple_of((a * 3 + b) * halo, 16)
        table[pl.ds(pl.multiple_of((zz + 1) * group + at, 16), halo), :] = rows

        @pl.when(zz == 0)
        def _():
            table[pl.ds(pl.multiple_of((nz + 1) * group + at, 16), halo), :] = rows

        @pl.when(zz == nz - 1)
        def _():
            table[pl.ds(at, halo), :] = rows

    rounds = [[(0, 0)]] + [[(s, -1), (s, 1)] for s in range(1, nz)]
    for r in range(nz + 2):
        landed_now = []
        if r < nz:
            for entry in rounds[r]:
                own_stage(entry, start)
                landed_now.append((entry, 1))
        if r == 0:
            edges(0, start)
        if r == nz - 1:
            edges(1, start)
        if 1 <= r <= nz:
            for entry in rounds[r - 1]:
                first_stage(entry, start)
                landed_now.append((entry, place.b_first))
        if r >= 2:
            for entry in rounds[r - 2]:
                second_stage(entry, start)
                landed_now.append((entry, place.b_second))
        for entry, b in landed_now:
            when(entry, functools.partial(fill, 0, b))
    for copy in weights + [own_basis]:
        copy.wait()
    rest = table.shape[0] - (nz + 2) * group
    table[(nz + 2) * group :, :] = jnp.zeros((rest, width), bf16)

    def project(o, carry):
        w_mix[o, :radial, :] = w1_ref[2 * width :, :]
        w_mix[o, radial:, :] = jnp.dot(
            g_ref[0, 1, o], w1_ref[width : 2 * width, :], preferred_element_type=f32
        ).astype(bf16)
        return carry

    lax.fori_loop(0, nz, project, 0)
    for a in range(1, na):
        for step in range(nz):

            def last(zz, a=a):
                for b in (1, place.b_first, place.b_second):
                    arrival(a, b, zz)
                    fill(a, b, zz)

            for entry in rounds[step]:
                when(entry, last)
    edges(0, lambda copy: copy.wait_recv())
    edges(1, lambda copy: copy.wait_recv())
    window = -(-3 * group // lanes) * lanes
    lane_s = lax.broadcasted_iota(jnp.int32, (slots, lanes), 1).astype(f32)
    sublane = lax.broadcasted_iota(jnp.int32, (atoms, slots), 0).astype(f32)

    def domain(o):
        position = jnp.broadcast_to(mg_ref[o, 0:1, :], (lanes, slots)).T
        target = jnp.broadcast_to(mg_ref[o, 1:2, :], (lanes, slots)).T
        own = g_ref[0, 1, o]
        pick = (position == lane_s).astype(bf16)
        source = jnp.dot(pick, own, preferred_element_type=f32)
        picks = jnp.concatenate(
            [(position - float(atoms + j * lanes) == lane_s).astype(bf16) for j in range(window // lanes)],
            axis=1,
        )
        rows = table[pl.ds(pl.multiple_of(o * group, 16), window), :]
        source = source + jnp.dot(picks, rows, preferred_element_type=f32)
        mix = jnp.concatenate([bg_ref[o], (target == lane_s).astype(bf16)], axis=1)
        pre = jnp.dot(source.astype(bf16), w1_ref[:width, :], preferred_element_type=f32)
        pre = pre + jnp.dot(mix, w_mix[o], preferred_element_type=f32)
        half = 0.5 * pre
        hidden = (half + half * jnp.tanh(half)).astype(bf16)
        incidence = (jnp.broadcast_to(mg_ref[o, 1:2, :], (atoms, slots)) == sublane).astype(bf16)
        summed = jnp.dot(incidence, hidden, preferred_element_type=f32).astype(bf16)
        return jnp.dot(summed, w2_ref[...], preferred_element_type=f32)

    def returned(step):
        device = place.along_z(step + 1)
        return remote(part_ref.at[step], landed.at[step], p_send.at[step], p_receive.at[step], device)

    def other(step, carry):
        part_ref[step] = domain(lax.rem(z + step + 1, nz)).astype(bf16)
        returned(step).start()
        return carry

    lax.fori_loop(0, nz - 1, other, 0)
    total = domain(z)
    for step in range(nz - 1):
        returned(step).wait_recv()
        total = total + landed[step].astype(f32)
    mean_square = jnp.mean(total * total, axis=-1, keepdims=True)
    normed = (total * lax.rsqrt(mean_square + 1e-05)).astype(bf16)
    update = jnp.dot(normed, w3_ref[...], preferred_element_type=f32)
    new_rows = (f_ref[...].astype(f32) + update).astype(bf16)
    edge_rows[...] = boundary(h_ref[0:1, :], new_rows)
    fresh[...] = new_rows
    keep = pltpu.make_async_copy(fresh, new_ref, local.at[0])
    keep.start()

    started = []
    written = []

    def begin(b, c, kind, slot, device):
        source = edge_rows if (b is None and c == 1) else n_ref.at[0, 1 if b is None else b, c]
        index = 1 if b is None else b
        copy = remote(source, n_ref.at[slot], n_send.at[kind, index, c], n_receive.at[slot], device)
        copy.start()
        started.append(copy)

    def landing(a, b, c):
        remote(n_ref.at[a, b, c], n_ref.at[a, b, c], n_send.at[0, 0, 0], n_receive.at[a, b, c], place.first).wait_recv()

    def write(a, b, c):
        copy = pltpu.make_async_copy(n_ref.at[a, b, c], out_ref.at[a, b, c], o_sem.at[a, b, c])
        copy.start()
        written.append(copy)

    def to_siblings_next(b, c):
        for i, device in enumerate(place.siblings):
            begin(b, c, 3 + i, (place.sibling_slot(i), 1 if b is None else b, c), device)

    begin(None, 1, 0, (0, 1, 0), place.along_z(1))
    begin(None, 1, 1, (0, 1, 2), place.along_z(-1))
    begin(None, 1, 2, (0, place.b_second, 1), place.first)
    to_siblings_next(None, 1)
    centre = pltpu.make_async_copy(edge_rows, out_ref.at[0, 1, 1], o_sem.at[0, 1, 1])
    centre.start()
    written.append(centre)
    order = (1, 0, 2)
    for c in order[1:]:
        landing(0, 1, c)
        begin(None, c, 2, (0, place.b_second, c), place.first)
        to_siblings_next(None, c)
        write(0, 1, c)
    for c in order:
        landing(0, place.b_first, c)
        begin(place.b_first, c, 2, (0, place.b_second, c), place.second)
        to_siblings_next(place.b_first, c)
        write(0, place.b_first, c)
    for c in order:
        landing(0, place.b_second, c)
        to_siblings_next(place.b_second, c)
        write(0, place.b_second, c)
    for b in (1, place.b_first, place.b_second):
        for a in range(1, na):
            for c in order:
                landing(a, b, c)
                write(a, b, c)
    for group_ in rounds:
        for entry in group_:
            own_stage(entry, finish)
            first_stage(entry, finish)
            second_stage(entry, finish)
    for q in range(2):
        edges(q, finish)
    for step in range(nz - 1):
        returned(step).wait_send()
    for copy in started:
        copy.wait_send()
    keep.wait()
    for copy in written:
        copy.wait()


def spread_kernel(new_ref, blocks_ref, new_out, out_ref, rows, blocks, row_sem, in_sem, out_sem):
    na = blocks_ref.shape[0]
    parts = (1, 0, 1) if na == 2 else (2, 0, 1)
    first = pltpu.make_async_copy(new_ref, rows, row_sem.at[0])
    last = pltpu.make_async_copy(rows, new_out, row_sem.at[1])
    loads = [
        (a, b, pltpu.make_async_copy(blocks_ref.at[a, b], blocks.at[a, b], in_sem.at[a, b]))
        for a in range(na)
        for b in range(3)
    ]
    for _, _, copy in loads:
        copy.start()
    first.start()
    stores = []
    for a, b, copy in loads:
        copy.wait()
        for part, slot in enumerate(parts):
            for c in range(3):
                cell = part * 9 + b * 3 + c
                if slot == a and cell != 13:
                    cell = cell - 1 if cell > 13 else cell
                    stores.append(pltpu.make_async_copy(blocks.at[a, b, c], out_ref.at[cell], out_sem.at[cell]))
                    stores[-1].start()
    first.wait()
    last.start()
    for copy in stores + [last]:
        copy.wait()


def shards(sizes, features, halo_index, edge_src, edge_dst, edge_count, edge_basis, w_edge_in, w_edge_out, w_update):
    nx, ny, nz = sizes
    atoms, width = features.shape
    groups, slots = edge_src.shape
    halo = halo_index.shape[0]
    radial = edge_basis.shape[1]
    hidden = w_edge_in.shape[2]
    lanes = -(-max(atoms, halo) // 128) * 128
    na = 2 if nx == 2 else 3
    f32, bf16 = jnp.float32, jnp.bfloat16
    basis = edge_basis.reshape(groups, slots, radial)
    vmem = pl.BlockSpec(memory_space=pltpu.VMEM)
    smem = pl.BlockSpec(memory_space=pltpu.SMEM)
    anywhere = pl.BlockSpec(memory_space=pl.ANY)
    dma = pltpu.SemaphoreType.DMA
    kinds = 4 + (na - 1)
    group = na * 3 * halo
    window = -(-3 * group // lanes) * lanes
    table_rows = (nz - 1) * group + window
    new_rows, blocks = pl.pallas_call(
        functools.partial(layer_kernel, sizes),
        out_shape=(
            jax.ShapeDtypeStruct((atoms, width), bf16),
            jax.ShapeDtypeStruct((na, 3, 3, halo, width), bf16),
        ),
        in_specs=[vmem, vmem, vmem, vmem, smem, anywhere, anywhere, anywhere, anywhere],
        out_specs=(anywhere, anywhere),
        scratch_shapes=[
            pltpu.VMEM((8, lanes), f32),
            pltpu.VMEM((nz, 8, slots), f32),
            pltpu.VMEM((na, 3, nz, atoms, width), bf16),
            pltpu.VMEM((na, 3, nz, 8, lanes), f32),
            pltpu.VMEM((nz, slots, radial), bf16),
            pltpu.VMEM((nz, 8, slots), f32),
            pltpu.VMEM(w_edge_in.shape[1:], bf16),
            pltpu.VMEM(w_edge_out.shape[1:], bf16),
            pltpu.VMEM(w_update.shape, bf16),
            pltpu.VMEM((table_rows, width), bf16),
            pltpu.VMEM((nz, radial + lanes, hidden), bf16),
            pltpu.VMEM((nz - 1, atoms, width), bf16),
            pltpu.VMEM((nz - 1, atoms, width), bf16),
            pltpu.VMEM((halo, width), bf16),
            pltpu.VMEM((atoms, width), bf16),
            pltpu.VMEM((na, 3, 3, halo, width), bf16),
            dma((2, kinds, 3, nz)),
            dma((2, na, 3, nz)),
            dma((2, nz)),
            dma((2, nz)),
            dma((4,)),
            dma((nz - 1,)),
            dma((nz - 1,)),
            dma((3 + na - 1, 3, 3)),
            dma((na, 3, 3)),
            dma((na, 3, 3)),
        ],
        compiler_params=pltpu.CompilerParams(
            collective_id=0, has_side_effects=True, vmem_limit_bytes=60 * 1024 * 1024
        ),
        name="layer",
    )(features, halo_index.reshape(1, halo), edge_src, edge_dst, edge_count, basis,
      w_edge_in[0], w_edge_out[0], w_update)
    return pl.pallas_call(
        spread_kernel,
        out_shape=(
            jax.ShapeDtypeStruct((atoms, width), bf16),
            jax.ShapeDtypeStruct((26, halo, width), bf16),
        ),
        in_specs=[anywhere, anywhere],
        out_specs=(anywhere, anywhere),
        scratch_shapes=[
            pltpu.VMEM((atoms, width), bf16),
            pltpu.VMEM((na, 3, 3, halo, width), bf16),
            dma((2,)),
            dma((na, 3)),
            dma((26,)),
        ],
        name="spread",
    )(new_rows, blocks)


def solution(mesh):
    sizes = tuple(mesh.shape[name] for name in AXES)
    in_specs = (
        P(AXES, None),
        P(AXES),
        P(AXES, None),
        P(AXES, None),
        P(AXES),
        P(AXES, None),
        P("gz", None, None),
        P("gz", None, None),
        P(),
    )
    out_specs = (P(AXES, None), P(AXES, None, None))
    return jax.shard_map(
        functools.partial(shards, sizes), mesh=mesh, in_specs=in_specs, out_specs=out_specs, check_vma=False
    )
```
